32 devices in a mesh: rep: 2 (over y), span: 2 (over x), seq: 4 (over z), head: 2 (over core).
Axes of the slice: x: 2, y: 2, z: 4, core: 2. Of those that a mesh axis runs over, the one named last changes fastest.
Arguments:
- queries: bfloat16 [4, 2, 1024, 4096], P(('rep', 'span'), 'head', None, 'seq'), parts along dimension 0, may hold values from -12 to 12
- keys: bfloat16 [4, 2, 1024, 4096], P(('rep', 'span'), 'head', None, 'seq'), parts along dimension 0, may hold values from -12 to 12
- values: bfloat16 [4, 2, 1024, 4096], P(('rep', 'span'), 'head', None, 'seq'), parts along dimension 0, may hold values from -6 to 6
- span_order: int32 [4], P('rep'), parts along dimension 0, may hold values from 0 to 15, as said below
Outputs:
- attention: bfloat16 [4, 2, 1024, 4096], P(('rep', 'span'), 'head', 'seq'), parts along dimension 0
The draws below stay inside these ranges and needn't reach their ends.
There are 2 independent parts, one for each index of `rep`. The reference program is written for one: setup_inputs(seed, part) draws one part's arguments, and reference() takes and returns one part's arrays. A program takes and returns all parts, laid end to end along the dimension named above; each array names one. Nothing has to cross between parts.
Inputs may be any that keep to these rules, and one draw needn't show every extreme that they name: `span_order`: each group has a different span index.
All inputs are finite; a program needn't handle non-finite values.
Results may differ from the reference program's by a relative error of at most 0.0055.
Values may be sent and summed in bfloat16 or wider, within the bound.
A program may use at most 128 MiB of HBM per device.

```python
import math
import jax
import jax.numpy as jnp
from jax import lax

HD = 128
HALF = 1024
GROUPS = 2
EMBED = 4096
N_HEAD = 2


def pair_draw(key):
    full_shape = (GROUPS, N_HEAD, HALF, EMBED)
    query_key = jax.random.fold_in(key, 11)
    key_key = jax.random.fold_in(key, 12)
    queries = jnp.clip(2.5 * jax.random.normal(query_key, full_shape, jnp.float32), -10.0, 10.0)
    keys = jnp.clip(jax.random.normal(key_key, full_shape, jnp.float32), -4.0, 4.0)
    return (queries, keys)


def draw_queries(key, part):
    return pair_draw(key)[0].astype(jnp.bfloat16)


def draw_keys(key, part):
    return pair_draw(key)[1].astype(jnp.bfloat16)


def draw_span_order(key, part):
    order_key = jax.random.fold_in(key, 21)
    shuffled = jax.random.permutation(order_key, jnp.arange(8 * GROUPS, dtype=jnp.int32))
    return shuffled[:GROUPS].astype(jnp.int32)


def level_of(rng, shape, pieces, smallest, largest):
    factor_of, own = 1.0, jax.random.fold_in(rng, 6)
    for position, shards_of in pieces:
        steps = jnp.exp(jax.random.uniform(jax.random.fold_in(own, position), (shards_of,), jnp.float32, smallest / len(pieces), largest / len(pieces)))
        factor_of = factor_of * jnp.repeat(steps, shape[position] // shards_of).reshape([-1 if axis == position else 1 for axis in range(len(shape))])
    return factor_of


def noise(own_key, shape, deviation, most, pieces=(), held_as=jnp.bfloat16):
    factor_of = level_of(own_key, shape, pieces, -0.22, 0.18) if pieces else 1.0
    entries = jax.random.normal(own_key, shape, jnp.float32) * deviation * factor_of
    return jnp.minimum(jnp.maximum(entries, -most), most).astype(held_as)


def setup_inputs(seed: int = 0, part: int = 0) -> dict:
    splits = jax.random.split(jax.random.key(seed), 5)
    own_keys = jax.random.split(jax.random.fold_in(splits[4], part), 5)
    queries = draw_queries(jax.random.fold_in(jax.random.fold_in(splits[4], part), 71), part)
    keys = draw_keys(jax.random.fold_in(jax.random.fold_in(splits[4], part), 71), part)
    values = noise(own_keys[2], (GROUPS, N_HEAD, HALF, EMBED), 1.0, 6.0, ((0, 2), (1, 2), (3, 4)))
    span_order = draw_span_order(jax.random.fold_in(jax.random.fold_in(splits[4], part), 71), part)
    return {"queries": queries, "keys": keys, "values": values, "span_order": span_order}


def reference(queries, keys, values, span_order):
    group_count = queries.shape[0]
    span_len = queries.shape[1] * queries.shape[2]
    embed_width = queries.shape[3]
    head_count = embed_width // HD
    score_scale = 1.0 / math.sqrt(HD)
    bias_rate = 1.0 / (2.0 * group_count)
    key_heads = keys.reshape(group_count * span_len, head_count, HD).transpose(1, 0, 2)
    value_heads = values.reshape(group_count * span_len, head_count, HD).transpose(1, 0, 2)
    key_spans = jnp.repeat(span_order, span_len)
    results = []
    for group in range(group_count):
        allowed = key_spans <= span_order[group]
        distance_bias = (span_order[group] - key_spans).astype(jnp.float32) * jnp.float32(bias_rate)

        def one_head(inputs):
            query_head, key_head, value_head = inputs
            scores = jnp.dot(query_head.astype(jnp.float32), key_head.astype(jnp.float32).T) * score_scale
            scores = scores - distance_bias[None, :]
            scores = jnp.where(allowed[None, :], scores, jnp.float32(-1e+30))
            row_max = lax.optimization_barrier(jnp.max(scores, axis=1, keepdims=True))
            weights = jnp.where(allowed[None, :], jnp.exp(scores - row_max), 0.0).astype(jnp.bfloat16)
            totals = lax.optimization_barrier(jnp.sum(weights.astype(jnp.float32), axis=1, keepdims=True))
            weighted = jnp.dot(weights.astype(jnp.float32), value_head.astype(jnp.float32))
            return (weighted / totals).astype(jnp.bfloat16)
        query_heads = queries[group].reshape(span_len, head_count, HD).transpose(1, 0, 2)
        result = lax.map(one_head, (query_heads, key_heads, value_heads))
        results.append(result.transpose(1, 0, 2).reshape(queries.shape[1], queries.shape[2], embed_width))
    return jnp.stack(results)
```

```python
import functools
import math

import jax
import jax.numpy as jnp
from jax import lax
from jax.experimental import pallas as pl
from jax.experimental.pallas import tpu as pltpu
from jax.sharding import PartitionSpec as P

HD = 128


def lookup(span_order, block_index):
    table = jnp.arange(span_order.shape[0], dtype=jnp.int32)
    return jnp.sum(
        jnp.where(block_index[:, None] == table[None, :], span_order[None, :], 0), axis=1
    )


def initial(query_heads):
    query_count = query_heads.shape[0]
    local_heads = query_heads.shape[1]
    return (
        jnp.full((local_heads, query_count), -1e30, jnp.float32),
        jnp.zeros((local_heads, query_count), jnp.float32),
        jnp.zeros((local_heads, query_count, HD), jnp.float32),
    )


def attend(running, query_heads, key_piece, value_piece, block_span, own_span, bias_rate):
    block_count = key_piece.shape[0]
    piece_rows = key_piece.shape[1]
    local_heads = key_piece.shape[2] // HD
    key_count = block_count * piece_rows
    score_scale = 1.0 / math.sqrt(HD)
    key_spans = jnp.repeat(block_span, piece_rows)
    allowed = key_spans <= own_span
    distance_bias = (own_span - key_spans).astype(jnp.float32) * jnp.float32(bias_rate)
    block_size = 1024
    block_total = key_count // block_size
    key_blocks = key_piece.reshape(block_total, block_size, local_heads, HD)
    value_blocks = value_piece.reshape(block_total, block_size, local_heads, HD)
    allow_blocks = allowed.reshape(block_total, block_size)
    bias_blocks = distance_bias.reshape(block_total, block_size)

    def advance(status, block_item):
        key_block, value_block, allow_block, bias_block = block_item
        maxima, totals, weighted = status
        scores = (
            jnp.einsum("qhd,khd->hqk", query_heads, key_block, preferred_element_type=jnp.float32)
            * score_scale
        )
        scores = scores - bias_block[None, None, :]
        scores = jnp.where(allow_block[None, None, :], scores, jnp.float32(-1e30))
        new_max = jnp.maximum(maxima, jnp.max(scores, axis=2))
        weights = jnp.where(
            allow_block[None, None, :], jnp.exp(scores - new_max[:, :, None]), 0.0
        ).astype(jnp.bfloat16)
        shrink = jnp.exp(maxima - new_max)
        totals = totals * shrink + jnp.sum(weights.astype(jnp.float32), axis=2)
        weighted = weighted * shrink[:, :, None] + jnp.einsum(
            "hqk,khd->hqd", weights, value_block, preferred_element_type=jnp.float32
        )
        return ((new_max, totals, weighted), None)

    running, unused = lax.scan(
        advance, running, (key_blocks, value_blocks, allow_blocks, bias_blocks)
    )
    return running


def finish(running):
    maxima, totals, weighted = running
    local_heads = weighted.shape[0]
    query_count = weighted.shape[1]
    output = (weighted / totals[:, :, None]).transpose(1, 0, 2)
    return output.reshape(1, 1, query_count, local_heads * HD).astype(jnp.bfloat16)


def per_device_general(queries, keys, values, span_order):
    half_rows = queries.shape[2]
    local_width = queries.shape[3]
    local_heads = local_width // HD
    halves = lax.axis_size("head")
    bias_rate = 1.0 / (2.0 * span_order.shape[0])
    own_span = lookup(span_order, jnp.reshape(lax.axis_index("span"), (1,)))[0]
    query_heads = queries.reshape(half_rows, local_heads, HD)
    pieces = (
        lax.all_gather(keys, ("span", "head"), axis=0, tiled=True),
        lax.all_gather(values, ("span", "head"), axis=0, tiled=True),
    )
    count = pieces[0].shape[0]
    block_index = jnp.arange(count, dtype=jnp.int32) // halves
    key_piece = pieces[0].reshape(count, half_rows, local_width)
    value_piece = pieces[1].reshape(count, half_rows, local_width)
    running = attend(
        initial(query_heads),
        query_heads,
        key_piece,
        value_piece,
        lookup(span_order, block_index),
        own_span,
        bias_rate,
    )
    result = finish(running)
    return lax.all_to_all(result, "seq", split_axis=2, concat_axis=3, tiled=True)


MESH = pl.DeviceIdType.MESH
ROWS = 256
CHUNK = 512
LAG = 4
ONES = 16
LOG2E = 1.4426950408889634
RATE = LOG2E / math.sqrt(HD)


def fused_kernel(
    heads, bias_rate, order_ref, q_in, k_in, v_in, out_ref,
    q, k, v, kp, vp, first, pay, pay_lse, px, px_lse, own, own_lse, stage, vt,
    cross_scores, own_scores, cross_weights, own_weights, cross_top, own_top,
    in_sem, p_send, p_recv, x_send, x_recv, l_send, l_recv, z_send, z_recv, keep_sem,
):
    rep, span = lax.axis_index("rep"), lax.axis_index("span")
    seq, core = lax.axis_index("seq"), lax.axis_index("head")
    partner = (rep, span, seq, 1 - core)
    across = (rep, 1 - span, seq, core)
    tokens, width = q.shape
    blocks = tokens // ROWS
    units = heads * blocks

    def cols(h):
        return pl.ds(pl.multiple_of(h * HD, HD), HD)

    def target(u):
        far = blocks - 1 - lax.rem(u, blocks)
        return 2 * lax.rem(seq // 2 + far // 2, 2) + lax.rem(seq + far, 2)

    def rows(u):
        return pl.ds(pl.multiple_of(target(u) * ROWS, ROWS), ROWS)

    def load(i, h):
        src, dst = ((q_in, q), (k_in, k), (v_in, v))[i]
        return pltpu.make_async_copy(src.at[:, cols(h)], dst.at[:, cols(h)], in_sem.at[i, h])

    def remote(src, dst, send, recv, device):
        return pltpu.make_async_remote_copy(
            src_ref=src, dst_ref=dst, send_sem=send, recv_sem=recv,
            device_id=device, device_id_type=MESH,
        )

    def to_partner(i, h):
        src, dst = ((k_in, kp), (v_in, vp))[i]
        return remote(
            src.at[:, cols(h)], dst.at[:, cols(h)], p_send.at[i, h], p_recv.at[i, h], partner
        )

    def first_slot(s):
        return remote(first.at[s], px.at[s], x_send.at[s], x_recv.at[s], across)

    def later_slot(u):
        s = u + LAG
        return remote(pay.at[u], px.at[s], x_send.at[s], x_recv.at[s], across)

    def lse_slot(u):
        return remote(pay_lse.at[u], px_lse.at[u + 1], l_send.at[u], l_recv.at[u], across)

    def out_cols(u):
        return pl.ds(pl.multiple_of(seq * width + (u // blocks) * HD, HD), HD)

    def to_seq(u):
        return remote(
            stage.at[u], out_ref.at[:, out_cols(u)], z_send.at[u], z_recv.at[u],
            (rep, span, target(u), core),
        )

    def to_self(u):
        return pltpu.make_async_copy(stage.at[u], out_ref.at[:, out_cols(u)], keep_sem.at[u // blocks])

    def start_loads(h, carry):
        for i in range(3):
            load(i, h).start()
        return carry

    lax.fori_loop(0, heads, start_loads, 0)

    barrier = pltpu.get_barrier_semaphore()
    peers = [partner, across]
    for far in range(1, blocks):
        there = 2 * lax.rem(seq // 2 + far // 2, 2) + lax.rem(seq + far, 2)
        peers.append((rep, span, there, core))
    for peer in peers:
        pl.semaphore_signal(barrier, inc=1, device_id=peer, device_id_type=MESH)

    load(0, 0).wait()
    for s in range(LAG):
        first[s] = q[rows(s), cols(0)].T
    pl.semaphore_wait(barrier, len(peers))

    first_slot(0).start()
    for i in range(2):
        to_partner(i, 0).start()
    for s in range(1, LAG):
        first_slot(s).start()

    def start_partner(h, carry):
        for i in range(2):
            to_partner(i, h).start()
        return carry

    lax.fori_loop(1, heads, start_partner, 0)

    difference = order_ref[span] - order_ref[1 - span]
    higher = jnp.minimum(jnp.maximum(difference, 0), 1).astype(jnp.float32)
    lower = 1.0 - higher
    shift = difference.astype(jnp.float32) * (bias_rate * LOG2E) * higher + lower * 1e30

    vt[:, HD:, :] = jnp.ones((heads, ONES, 2 * tokens), jnp.bfloat16)

    def turn_values(h, t):
        here = pl.ds(pl.multiple_of(t * ROWS, ROWS), ROWS)
        there = pl.ds(pl.multiple_of(tokens + t * ROWS, ROWS), ROWS)
        vt[h, :HD, here] = v[here, cols(h)].T
        vt[h, :HD, there] = vp[here, cols(h)].T

    load(2, 0).wait()
    to_partner(1, 0).wait_recv()
    for t in range(blocks):
        turn_values(0, t)

    def score(h, scores_ref, dot):
        top = None
        for c in range(2 * tokens // CHUNK):
            source = k if c * CHUNK < tokens else kp
            part = dot(source[pl.ds((c * CHUNK) % tokens, CHUNK), cols(h)])
            scores_ref[pl.ds(c * CHUNK, CHUNK), :] = part
            part_top = jnp.max(part, axis=0, keepdims=True)
            top = part_top if top is None else jnp.maximum(top, part_top)
        return top * RATE

    def weigh(scores_ref, weights_ref, top):
        for c in range(2 * tokens // CHUNK):
            part = pl.ds(c * CHUNK, CHUNK)
            weights_ref[part, :] = jnp.exp2(scores_ref[part, :] * RATE - top).astype(jnp.bfloat16)

    def gather(h, weights_ref, top):
        total = jnp.dot(vt[h], weights_ref[...], preferred_element_type=jnp.float32)
        sums = total[HD : HD + 1]
        return total[:HD] * (1.0 / sums), top + jnp.log2(sums)

    def merge(s):
        u = jnp.maximum(s - LAG, 0)
        near_lse, far_lse = own_lse[u], px_lse[jnp.maximum(s - LAG + 1, 0)] - shift
        top = jnp.maximum(near_lse, far_lse)
        near_part, far_part = jnp.exp2(near_lse - top), jnp.exp2(far_lse - top)
        scale = 1.0 / (near_part + far_part)
        mixed = own[u] * (near_part * scale) + px[s].astype(jnp.float32) * (far_part * scale)
        stage[u] = mixed.T.astype(jnp.bfloat16)

    def await_slot(s):
        remote(first.at[0], px.at[s], x_send.at[s], x_recv.at[s], across).wait_recv()

        @pl.when(s >= LAG)
        def with_lse():
            lse_slot(s - LAG).wait_recv()

    def pass_on(u):
        @pl.when(lax.rem(u, blocks) < blocks - 1)
        def away():
            to_seq(u).start()

        @pl.when(lax.rem(u, blocks) == blocks - 1)
        def here():
            to_self(u).start()

    def step(s, carry):
        unit = jnp.minimum(s, units - 1)
        before = jnp.maximum(s - 1, 0)
        h, t = unit // blocks, lax.rem(s, blocks)
        h_before = before // blocks
        h_next = jnp.minimum(h + 1, heads - 1)
        await_slot(s)

        @pl.when(jnp.logical_and(t == 0, s < units))
        def await_head():
            load(1, h).wait()
            to_partner(0, h).wait_recv()

            @pl.when(h + 1 < heads)
            def next_head():
                load(0, h + 1).wait()
                load(2, h + 1).wait()
                to_partner(1, h + 1).wait_recv()

        result, lse = gather(h_before, cross_weights, cross_top[...])
        weigh(own_scores, own_weights, own_top[...])
        query_block = px[s]
        top = score(
            h, cross_scores,
            lambda key: jnp.dot(key, query_block, preferred_element_type=jnp.float32),
        )
        cross_top[...] = top
        ahead = jnp.minimum(before + LAG, units - 1)
        turned = q[rows(ahead), cols(ahead // blocks)].T.astype(jnp.float32)
        pay[before] = (turned * higher + result * lower).astype(jnp.bfloat16)
        pay_lse[before] = lse

        merge(s)

        result, lse = gather(h_before, own_weights, own_top[...])
        own[before] = result
        own_lse[before] = lse
        weigh(cross_scores, cross_weights, top)
        own_query = q[rows(unit), cols(h)]
        own_top[...] = score(
            h, own_scores,
            lambda key: lax.dot_general(
                key, own_query, (((1,), (1,)), ((), ())), preferred_element_type=jnp.float32
            ),
        )
        turn_values(h_next, t)

        @pl.when(s > 0)
        def answer():
            later_slot(before).start()
            lse_slot(before).start()

        @pl.when(s >= LAG)
        def finished():
            pass_on(s - LAG)

        return carry

    lax.fori_loop(0, units + 1, step, 0)

    def complete(s, carry):
        await_slot(s)
        merge(s)
        pass_on(s - LAG)
        return carry

    lax.fori_loop(units + 1, units + LAG, complete, 0)

    def drain_first(s, carry):
        first_slot(s).wait_send()
        return carry

    lax.fori_loop(0, LAG, drain_first, 0)

    def drain(u, carry):
        later_slot(u).wait_send()
        lse_slot(u).wait_send()

        @pl.when(lax.rem(u, blocks) < blocks - 1)
        def away():
            to_seq(u).wait_send()
            to_seq(u).wait_recv()

        @pl.when(lax.rem(u, blocks) == blocks - 1)
        def here():
            to_self(u).wait()

        return carry

    lax.fori_loop(0, units, drain, 0)

    def drain_partner(h, carry):
        for i in range(2):
            to_partner(i, h).wait_send()
        return carry

    lax.fori_loop(0, heads, drain_partner, 0)


def per_device_fused(queries, keys, values, span_order):
    tokens, width = queries.shape[2], queries.shape[3]
    heads = width // HD
    seq_count = lax.axis_size("seq")
    blocks = tokens // ROWS
    units = heads * blocks
    slots = units + LAG
    bias_rate = 1.0 / (2.0 * span_order.shape[0])
    query, key, value = (a.reshape(tokens, width) for a in (queries, keys, values))
    far = pl.BlockSpec(memory_space=pl.ANY)
    dma = pltpu.SemaphoreType.DMA

    def half(*shape):
        return pltpu.VMEM(shape, jnp.bfloat16)

    def full(*shape):
        return pltpu.VMEM(shape, jnp.float32)

    result = pl.pallas_call(
        functools.partial(fused_kernel, heads, bias_rate),
        out_shape=jax.ShapeDtypeStruct((tokens // seq_count, width * seq_count), jnp.bfloat16),
        in_specs=[pl.BlockSpec(memory_space=pltpu.SMEM), far, far, far],
        out_specs=far,
        scratch_shapes=[half(tokens, width)] * 5
        + [half(LAG, HD, ROWS), half(units, HD, ROWS), full(units, 1, ROWS)]
        + [half(slots, HD, ROWS), full(units + 1, 1, ROWS)]
        + [full(units, HD, ROWS), full(units, 1, ROWS), half(units, ROWS, HD)]
        + [half(heads, HD + ONES, 2 * tokens)]
        + [full(2 * tokens, ROWS)] * 2
        + [half(2 * tokens, ROWS)] * 2
        + [full(1, ROWS)] * 2
        + [dma((3, heads)), dma((2, heads)), dma((2, heads)), dma((slots,)), dma((slots,))]
        + [dma((units,))] * 4
        + [dma((heads,))],
        compiler_params=pltpu.CompilerParams(
            collective_id=0, has_side_effects=True, vmem_limit_bytes=60 * 1024 * 1024
        ),
    )(span_order, query, key, value)
    return result.reshape(1, 1, tokens // seq_count, width * seq_count)


def per_device(queries, keys, values, span_order):
    tokens = queries.shape[2]
    seq_count = lax.axis_size("seq")
    fits = (
        lax.axis_size("span") == 2
        and lax.axis_size("head") == 2
        and seq_count == 4
        and tokens == seq_count * ROWS
        and queries.shape[3] % HD == 0
    )
    run = per_device_fused if fits else per_device_general
    return run(queries, keys, values, span_order)


def solution(mesh):
    return jax.shard_map(
        per_device,
        mesh=mesh,
        in_specs=(
            P(("rep", "span"), "head", None, "seq"),
            P(("rep", "span"), "head", None, "seq"),
            P(("rep", "span"), "head", None, "seq"),
            P("rep"),
        ),
        out_specs=P(("rep", "span"), "head", "seq", None),
        check_vma=False,
    )
```

```python
import functools
import math

import jax
import jax.numpy as jnp
from jax import lax
from jax.experimental import pallas as pl
from jax.experimental.pallas import tpu as pltpu
from jax.sharding import PartitionSpec as P

HD = 128


def lookup(span_order, block_index):
    table = jnp.arange(span_order.shape[0], dtype=jnp.int32)
    return jnp.sum(
        jnp.where(block_index[:, None] == table[None, :], span_order[None, :], 0), axis=1
    )


def initial(query_heads):
    query_count = query_heads.shape[0]
    local_heads = query_heads.shape[1]
    return (
        jnp.full((local_heads, query_count), -1e30, jnp.float32),
        jnp.zeros((local_heads, query_count), jnp.float32),
        jnp.zeros((local_heads, query_count, HD), jnp.float32),
    )


def attend(running, query_heads, key_piece, value_piece, block_span, own_span, bias_rate):
    block_count = key_piece.shape[0]
    piece_rows = key_piece.shape[1]
    local_heads = key_piece.shape[2] // HD
    key_count = block_count * piece_rows
    score_scale = 1.0 / math.sqrt(HD)
    key_spans = jnp.repeat(block_span, piece_rows)
    allowed = key_spans <= own_span
    distance_bias = (own_span - key_spans).astype(jnp.float32) * jnp.float32(bias_rate)
    block_size = 1024
    block_total = key_count // block_size
    key_blocks = key_piece.reshape(block_total, block_size, local_heads, HD)
    value_blocks = value_piece.reshape(block_total, block_size, local_heads, HD)
    allow_blocks = allowed.reshape(block_total, block_size)
    bias_blocks = distance_bias.reshape(block_total, block_size)

    def advance(status, block_item):
        key_block, value_block, allow_block, bias_block = block_item
        maxima, totals, weighted = status
        scores = (
            jnp.einsum("qhd,khd->hqk", query_heads, key_block, preferred_element_type=jnp.float32)
            * score_scale
        )
        scores = scores - bias_block[None, None, :]
        scores = jnp.where(allow_block[None, None, :], scores, jnp.float32(-1e30))
        new_max = jnp.maximum(maxima, jnp.max(scores, axis=2))
        weights = jnp.where(
            allow_block[None, None, :], jnp.exp(scores - new_max[:, :, None]), 0.0
        ).astype(jnp.bfloat16)
        shrink = jnp.exp(maxima - new_max)
        totals = totals * shrink + jnp.sum(weights.astype(jnp.float32), axis=2)
        weighted = weighted * shrink[:, :, None] + jnp.einsum(
            "hqk,khd->hqd", weights, value_block, preferred_element_type=jnp.float32
        )
        return ((new_max, totals, weighted), None)

    running, unused = lax.scan(
        advance, running, (key_blocks, value_blocks, allow_blocks, bias_blocks)
    )
    return running


def finish(running):
    maxima, totals, weighted = running
    local_heads = weighted.shape[0]
    query_count = weighted.shape[1]
    output = (weighted / totals[:, :, None]).transpose(1, 0, 2)
    return output.reshape(1, 1, query_count, local_heads * HD).astype(jnp.bfloat16)


def per_device_general(queries, keys, values, span_order):
    half_rows = queries.shape[2]
    local_width = queries.shape[3]
    local_heads = local_width // HD
    halves = lax.axis_size("head")
    bias_rate = 1.0 / (2.0 * span_order.shape[0])
    own_span = lookup(span_order, jnp.reshape(lax.axis_index("span"), (1,)))[0]
    query_heads = queries.reshape(half_rows, local_heads, HD)
    pieces = (
        lax.all_gather(keys, ("span", "head"), axis=0, tiled=True),
        lax.all_gather(values, ("span", "head"), axis=0, tiled=True),
    )
    count = pieces[0].shape[0]
    block_index = jnp.arange(count, dtype=jnp.int32) // halves
    key_piece = pieces[0].reshape(count, half_rows, local_width)
    value_piece = pieces[1].reshape(count, half_rows, local_width)
    running = attend(
        initial(query_heads),
        query_heads,
        key_piece,
        value_piece,
        lookup(span_order, block_index),
        own_span,
        bias_rate,
    )
    result = finish(running)
    return lax.all_to_all(result, "seq", split_axis=2, concat_axis=3, tiled=True)


MESH = pl.DeviceIdType.MESH
ROWS = 256
CHUNK = 256
LAG = 4
ONES = 16
LOG2E = 1.4426950408889634
RATE = LOG2E / math.sqrt(HD)


def fused_kernel(
    heads, bias_rate, order_ref, q_in, k_in, v_in, out_ref,
    q, k, v, kp, vp, first, pay, pay_lse, px, px_lse, own, own_lse, stage, vt,
    scores, weights, cross_top, own_top,
    in_sem, p_send, p_recv, x_send, x_recv, l_send, l_recv, z_send, z_recv, keep_sem,
):
    rep, span = lax.axis_index("rep"), lax.axis_index("span")
    seq, core = lax.axis_index("seq"), lax.axis_index("head")
    partner = (rep, span, seq, 1 - core)
    across = (rep, 1 - span, seq, core)
    tokens, width = q.shape
    blocks = tokens // ROWS
    units = heads * blocks

    def cols(h):
        return pl.ds(pl.multiple_of(h * HD, HD), HD)

    def target(u):
        far = blocks - 1 - lax.rem(u, blocks)
        return 2 * lax.rem(seq // 2 + far // 2, 2) + lax.rem(seq + far, 2)

    def rows(u):
        return pl.ds(pl.multiple_of(target(u) * ROWS, ROWS), ROWS)

    def load(i, h):
        src, dst = ((q_in, q), (k_in, k), (v_in, v))[i]
        return pltpu.make_async_copy(src.at[:, cols(h)], dst.at[:, cols(h)], in_sem.at[i, h])

    def remote(src, dst, send, recv, device):
        return pltpu.make_async_remote_copy(
            src_ref=src, dst_ref=dst, send_sem=send, recv_sem=recv,
            device_id=device, device_id_type=MESH,
        )

    def to_partner(i, h):
        src, dst = ((k_in, kp), (v_in, vp))[i]
        return remote(
            src.at[:, cols(h)], dst.at[:, cols(h)], p_send.at[i, h], p_recv.at[i, h], partner
        )

    def first_slot(s):
        return remote(first.at[s], px.at[s], x_send.at[s], x_recv.at[s], across)

    def later_slot(u):
        s = u + LAG
        return remote(pay.at[u], px.at[s], x_send.at[s], x_recv.at[s], across)

    def lse_slot(u):
        return remote(pay_lse.at[u], px_lse.at[u + 1], l_send.at[u], l_recv.at[u], across)

    def out_cols(u):
        return pl.ds(pl.multiple_of(seq * width + (u // blocks) * HD, HD), HD)

    def to_seq(u):
        return remote(
            stage.at[u], out_ref.at[:, out_cols(u)], z_send.at[u], z_recv.at[u],
            (rep, span, target(u), core),
        )

    def to_self(u):
        return pltpu.make_async_copy(stage.at[u], out_ref.at[:, out_cols(u)], keep_sem.at[u // blocks])

    def start_loads(h, carry):
        for i in range(3):
            load(i, h).start()
        return carry

    lax.fori_loop(0, heads, start_loads, 0)

    barrier = pltpu.get_barrier_semaphore()
    peers = [partner, across]
    for far in range(1, blocks):
        there = 2 * lax.rem(seq // 2 + far // 2, 2) + lax.rem(seq + far, 2)
        peers.append((rep, span, there, core))
    for peer in peers:
        pl.semaphore_signal(barrier, inc=1, device_id=peer, device_id_type=MESH)

    load(0, 0).wait()
    for s in range(LAG):
        first[s] = q[rows(s), cols(0)].T
    pl.semaphore_wait(barrier, len(peers))

    first_slot(0).start()
    for i in range(2):
        to_partner(i, 0).start()
    for s in range(1, LAG):
        first_slot(s).start()

    def start_partner(h, carry):
        for i in range(2):
            to_partner(i, h).start()
        return carry

    lax.fori_loop(1, heads, start_partner, 0)

    difference = order_ref[span] - order_ref[1 - span]
    higher = jnp.minimum(jnp.maximum(difference, 0), 1).astype(jnp.float32)
    lower = 1.0 - higher
    shift = difference.astype(jnp.float32) * (bias_rate * LOG2E) * higher + lower * 1e30

    vt[:, HD:, :] = jnp.ones((heads, ONES, 2 * tokens), jnp.bfloat16)

    def turn_values(h, t):
        here = pl.ds(pl.multiple_of(t * ROWS, ROWS), ROWS)
        there = pl.ds(pl.multiple_of(tokens + t * ROWS, ROWS), ROWS)
        vt[h, :HD, here] = v[here, cols(h)].T
        vt[h, :HD, there] = vp[here, cols(h)].T

    load(2, 0).wait()
    to_partner(1, 0).wait_recv()
    for t in range(blocks):
        turn_values(0, t)

    def advance(h, dot, shift):
        tops = []
        for c in range(2 * tokens // CHUNK):
            part = pl.ds(c * CHUNK, CHUNK)
            weights[part, :] = jnp.exp2(scores[part, :] * RATE - shift).astype(jnp.bfloat16)
            source = k if c * CHUNK < tokens else kp
            fresh = dot(source[pl.ds((c * CHUNK) % tokens, CHUNK), cols(h)])
            scores[part, :] = fresh
            tops.append(jnp.max(fresh, axis=0, keepdims=True))
        return functools.reduce(jnp.maximum, tops) * RATE

    def gather(h, top):
        total = jnp.dot(vt[h], weights[...], preferred_element_type=jnp.float32)
        sums = total[HD : HD + 1]
        return total[:HD] * (1.0 / sums), top + jnp.log2(sums)

    def merge(s):
        u = jnp.maximum(s - LAG, 0)
        near_lse, far_lse = own_lse[u], px_lse[jnp.maximum(s - LAG + 1, 0)] - shift
        top = jnp.maximum(near_lse, far_lse)
        near_part, far_part = jnp.exp2(near_lse - top), jnp.exp2(far_lse - top)
        scale = 1.0 / (near_part + far_part)
        mixed = own[u] * (near_part * scale) + px[s].astype(jnp.float32) * (far_part * scale)
        stage[u] = mixed.T.astype(jnp.bfloat16)

    def await_slot(s):
        remote(first.at[0], px.at[s], x_send.at[s], x_recv.at[s], across).wait_recv()

        @pl.when(s >= LAG)
        def with_lse():
            lse_slot(s - LAG).wait_recv()

    def pass_on(u):
        @pl.when(lax.rem(u, blocks) < blocks - 1)
        def away():
            to_seq(u).start()

        @pl.when(lax.rem(u, blocks) == blocks - 1)
        def here():
            to_self(u).start()

    def step(s, carry):
        unit = jnp.minimum(s, units - 1)
        before = jnp.maximum(s - 1, 0)
        h, t = unit // blocks, lax.rem(s, blocks)
        h_before = before // blocks
        h_next = jnp.minimum(h + 1, heads - 1)
        await_slot(s)

        @pl.when(jnp.logical_and(t == 0, s < units))
        def await_head():
            load(1, h).wait()
            to_partner(0, h).wait_recv()

            @pl.when(h + 1 < heads)
            def next_head():
                load(0, h + 1).wait()
                load(2, h + 1).wait()
                to_partner(1, h + 1).wait_recv()

        result, lse = gather(h_before, cross_top[...])
        query_block = px[s]
        cross_top[...] = advance(
            h,
            lambda key: jnp.dot(key, query_block, preferred_element_type=jnp.float32),
            own_top[...],
        )
        ahead = jnp.minimum(before + LAG, units - 1)
        turned = q[rows(ahead), cols(ahead // blocks)].T.astype(jnp.float32)
        pay[before] = (turned * higher + result * lower).astype(jnp.bfloat16)
        pay_lse[before] = lse

        @pl.when(s > 0)
        def answer():
            later_slot(before).start()
            lse_slot(before).start()

        merge(s)
        result, lse = gather(h_before, own_top[...])
        own[before] = result
        own_lse[before] = lse
        own_query = q[rows(unit), cols(h)]
        own_top[...] = advance(
            h,
            lambda key: lax.dot_general(
                key, own_query, (((1,), (1,)), ((), ())), preferred_element_type=jnp.float32
            ),
            cross_top[...],
        )
        turn_values(h_next, t)

        @pl.when(s >= LAG)
        def finished():
            pass_on(s - LAG)

        return carry

    lax.fori_loop(0, units + 1, step, 0)

    def complete(s, carry):
        await_slot(s)
        merge(s)
        pass_on(s - LAG)
        return carry

    lax.fori_loop(units + 1, units + LAG, complete, 0)

    def drain_first(s, carry):
        first_slot(s).wait_send()
        return carry

    lax.fori_loop(0, LAG, drain_first, 0)

    def drain(u, carry):
        later_slot(u).wait_send()
        lse_slot(u).wait_send()

        @pl.when(lax.rem(u, blocks) < blocks - 1)
        def away():
            to_seq(u).wait_send()
            to_seq(u).wait_recv()

        @pl.when(lax.rem(u, blocks) == blocks - 1)
        def here():
            to_self(u).wait()

        return carry

    lax.fori_loop(0, units, drain, 0)

    def drain_partner(h, carry):
        for i in range(2):
            to_partner(i, h).wait_send()
        return carry

    lax.fori_loop(0, heads, drain_partner, 0)


def per_device_fused(queries, keys, values, span_order):
    tokens, width = queries.shape[2], queries.shape[3]
    heads = width // HD
    seq_count = lax.axis_size("seq")
    blocks = tokens // ROWS
    units = heads * blocks
    slots = units + LAG
    bias_rate = 1.0 / (2.0 * span_order.shape[0])
    query, key, value = (a.reshape(tokens, width) for a in (queries, keys, values))
    far = pl.BlockSpec(memory_space=pl.ANY)
    dma = pltpu.SemaphoreType.DMA

    def half(*shape):
        return pltpu.VMEM(shape, jnp.bfloat16)

    def full(*shape):
        return pltpu.VMEM(shape, jnp.float32)

    result = pl.pallas_call(
        functools.partial(fused_kernel, heads, bias_rate),
        out_shape=jax.ShapeDtypeStruct((tokens // seq_count, width * seq_count), jnp.bfloat16),
        in_specs=[pl.BlockSpec(memory_space=pltpu.SMEM), far, far, far],
        out_specs=far,
        scratch_shapes=[half(tokens, width)] * 5
        + [half(LAG, HD, ROWS), half(units, HD, ROWS), full(units, 1, ROWS)]
        + [half(slots, HD, ROWS), full(units + 1, 1, ROWS)]
        + [full(units, HD, ROWS), full(units, 1, ROWS), half(units, ROWS, HD)]
        + [half(heads, HD + ONES, 2 * tokens)]
        + [full(2 * tokens, ROWS)]
        + [half(2 * tokens, ROWS)]
        + [full(1, ROWS)] * 2
        + [dma((3, heads)), dma((2, heads)), dma((2, heads)), dma((slots,)), dma((slots,))]
        + [dma((units,))] * 4
        + [dma((heads,))],
        compiler_params=pltpu.CompilerParams(
            collective_id=0, has_side_effects=True, vmem_limit_bytes=60 * 1024 * 1024
        ),
    )(span_order, query, key, value)
    return result.reshape(1, 1, tokens // seq_count, width * seq_count)


def per_device(queries, keys, values, span_order):
    tokens = queries.shape[2]
    seq_count = lax.axis_size("seq")
    fits = (
        lax.axis_size("span") == 2
        and lax.axis_size("head") == 2
        and seq_count == 4
        and tokens == seq_count * ROWS
        and queries.shape[3] % HD == 0
    )
    run = per_device_fused if fits else per_device_general
    return run(queries, keys, values, span_order)


def solution(mesh):
    return jax.shard_map(
        per_device,
        mesh=mesh,
        in_specs=(
            P(("rep", "span"), "head", None, "seq"),
            P(("rep", "span"), "head", None, "seq"),
            P(("rep", "span"), "head", None, "seq"),
            P("rep"),
        ),
        out_specs=P(("rep", "span"), "head", "seq", None),
        check_vma=False,
    )
```

```python
import functools
import math

import jax
import jax.numpy as jnp
from jax import lax
from jax.experimental import pallas as pl
from jax.experimental.pallas import tpu as pltpu
from jax.sharding import PartitionSpec as P

HD = 128


def lookup(span_order, block_index):
    table = jnp.arange(span_order.shape[0], dtype=jnp.int32)
    return jnp.sum(
        jnp.where(block_index[:, None] == table[None, :], span_order[None, :], 0), axis=1
    )


def initial(query_heads):
    query_count = query_heads.shape[0]
    local_heads = query_heads.shape[1]
    return (
        jnp.full((local_heads, query_count), -1e30, jnp.float32),
        jnp.zeros((local_heads, query_count), jnp.float32),
        jnp.zeros((local_heads, query_count, HD), jnp.float32),
    )


def attend(running, query_heads, key_piece, value_piece, block_span, own_span, bias_rate):
    block_count = key_piece.shape[0]
    piece_rows = key_piece.shape[1]
    local_heads = key_piece.shape[2] // HD
    key_count = block_count * piece_rows
    score_scale = 1.0 / math.sqrt(HD)
    key_spans = jnp.repeat(block_span, piece_rows)
    allowed = key_spans <= own_span
    distance_bias = (own_span - key_spans).astype(jnp.float32) * jnp.float32(bias_rate)
    block_size = 1024
    block_total = key_count // block_size
    key_blocks = key_piece.reshape(block_total, block_size, local_heads, HD)
    value_blocks = value_piece.reshape(block_total, block_size, local_heads, HD)
    allow_blocks = allowed.reshape(block_total, block_size)
    bias_blocks = distance_bias.reshape(block_total, block_size)

    def advance(status, block_item):
        key_block, value_block, allow_block, bias_block = block_item
        maxima, totals, weighted = status
        scores = (
            jnp.einsum("qhd,khd->hqk", query_heads, key_block, preferred_element_type=jnp.float32)
            * score_scale
        )
        scores = scores - bias_block[None, None, :]
        scores = jnp.where(allow_block[None, None, :], scores, jnp.float32(-1e30))
        new_max = jnp.maximum(maxima, jnp.max(scores, axis=2))
        weights = jnp.where(
            allow_block[None, None, :], jnp.exp(scores - new_max[:, :, None]), 0.0
        ).astype(jnp.bfloat16)
        shrink = jnp.exp(maxima - new_max)
        totals = totals * shrink + jnp.sum(weights.astype(jnp.float32), axis=2)
        weighted = weighted * shrink[:, :, None] + jnp.einsum(
            "hqk,khd->hqd", weights, value_block, preferred_element_type=jnp.float32
        )
        return ((new_max, totals, weighted), None)

    running, unused = lax.scan(
        advance, running, (key_blocks, value_blocks, allow_blocks, bias_blocks)
    )
    return running


def finish(running):
    maxima, totals, weighted = running
    local_heads = weighted.shape[0]
    query_count = weighted.shape[1]
    output = (weighted / totals[:, :, None]).transpose(1, 0, 2)
    return output.reshape(1, 1, query_count, local_heads * HD).astype(jnp.bfloat16)


def per_device_general(queries, keys, values, span_order):
    half_rows = queries.shape[2]
    local_width = queries.shape[3]
    local_heads = local_width // HD
    halves = lax.axis_size("head")
    bias_rate = 1.0 / (2.0 * span_order.shape[0])
    own_span = lookup(span_order, jnp.reshape(lax.axis_index("span"), (1,)))[0]
    query_heads = queries.reshape(half_rows, local_heads, HD)
    pieces = (
        lax.all_gather(keys, ("span", "head"), axis=0, tiled=True),
        lax.all_gather(values, ("span", "head"), axis=0, tiled=True),
    )
    count = pieces[0].shape[0]
    block_index = jnp.arange(count, dtype=jnp.int32) // halves
    key_piece = pieces[0].reshape(count, half_rows, local_width)
    value_piece = pieces[1].reshape(count, half_rows, local_width)
    running = attend(
        initial(query_heads),
        query_heads,
        key_piece,
        value_piece,
        lookup(span_order, block_index),
        own_span,
        bias_rate,
    )
    result = finish(running)
    return lax.all_to_all(result, "seq", split_axis=2, concat_axis=3, tiled=True)


MESH = pl.DeviceIdType.MESH
ROWS = 256
CHUNK = 256
LAG = 4
ONES = 16
LOG2E = 1.4426950408889634
RATE = LOG2E / math.sqrt(HD)


def fused_kernel(
    heads, bias_rate, order_ref, q_in, k_in, v_in, out_ref,
    q, k, v, kp, vp, first, pay, pay_lse, px, px_lse, own, own_lse, stage, vt,
    scores, weights, cross_top, own_top,
    in_sem, p_send, p_recv, x_send, x_recv, l_send, l_recv, z_send, z_recv, keep_sem,
):
    rep, span = lax.axis_index("rep"), lax.axis_index("span")
    seq, core = lax.axis_index("seq"), lax.axis_index("head")
    partner = (rep, span, seq, 1 - core)
    across = (rep, 1 - span, seq, core)
    tokens, width = q.shape
    blocks = tokens // ROWS
    units = heads * blocks

    def cols(h):
        return pl.ds(pl.multiple_of(h * HD, HD), HD)

    def target(u):
        far = blocks - 1 - lax.rem(u, blocks)
        return 2 * lax.rem(seq // 2 + far // 2, 2) + lax.rem(seq + far, 2)

    def rows(u):
        return pl.ds(pl.multiple_of(target(u) * ROWS, ROWS), ROWS)

    def load(i, h):
        src, dst = ((q_in, q), (k_in, k), (v_in, v))[i]
        return pltpu.make_async_copy(src.at[:, cols(h)], dst.at[:, cols(h)], in_sem.at[i, h])

    def remote(src, dst, send, recv, device):
        return pltpu.make_async_remote_copy(
            src_ref=src, dst_ref=dst, send_sem=send, recv_sem=recv,
            device_id=device, device_id_type=MESH,
        )

    def to_partner(i, h):
        src, dst = ((k_in, kp), (v_in, vp))[i]
        return remote(
            src.at[:, cols(h)], dst.at[:, cols(h)], p_send.at[i, h], p_recv.at[i, h], partner
        )

    def first_slot(s):
        return remote(first.at[s], px.at[s], x_send.at[s], x_recv.at[s], across)

    def later_slot(u):
        s = u + LAG
        return remote(pay.at[u], px.at[s], x_send.at[s], x_recv.at[s], across)

    def lse_slot(u):
        return remote(pay_lse.at[u], px_lse.at[u + 1], l_send.at[u], l_recv.at[u], across)

    def out_cols(u):
        return pl.ds(pl.multiple_of(seq * width + (u // blocks) * HD, HD), HD)

    def to_seq(u):
        return remote(
            stage.at[u], out_ref.at[:, out_cols(u)], z_send.at[u], z_recv.at[u],
            (rep, span, target(u), core),
        )

    def to_self(u):
        return pltpu.make_async_copy(stage.at[u], out_ref.at[:, out_cols(u)], keep_sem.at[u // blocks])

    def start_loads(h, carry):
        for i in range(3):
            load(i, h).start()
        return carry

    lax.fori_loop(0, heads, start_loads, 0)

    barrier = pltpu.get_barrier_semaphore()
    peers = [partner, across]
    for far in range(1, blocks):
        there = 2 * lax.rem(seq // 2 + far // 2, 2) + lax.rem(seq + far, 2)
        peers.append((rep, span, there, core))
    for peer in peers:
        pl.semaphore_signal(barrier, inc=1, device_id=peer, device_id_type=MESH)

    load(0, 0).wait()
    for s in range(LAG):
        first[s] = q[rows(s), cols(0)].T
    pl.semaphore_wait(barrier, len(peers))

    first_slot(0).start()
    for i in range(2):
        to_partner(i, 0).start()
    for s in range(1, LAG):
        first_slot(s).start()

    def start_partner(h, carry):
        for i in range(2):
            to_partner(i, h).start()
        return carry

    lax.fori_loop(1, heads, start_partner, 0)

    difference = order_ref[span] - order_ref[1 - span]
    higher = jnp.minimum(jnp.maximum(difference, 0), 1).astype(jnp.float32)
    lower = 1.0 - higher
    shift = difference.astype(jnp.float32) * (bias_rate * LOG2E) * higher + lower * 1e30

    vt[:, HD:, :] = jnp.ones((heads, ONES, 2 * tokens), jnp.bfloat16)

    def turn_values(h, t):
        here = pl.ds(pl.multiple_of(t * ROWS, ROWS), ROWS)
        there = pl.ds(pl.multiple_of(tokens + t * ROWS, ROWS), ROWS)
        vt[h, :HD, here] = v[here, cols(h)].T
        vt[h, :HD, there] = vp[here, cols(h)].T

    load(2, 0).wait()
    to_partner(1, 0).wait_recv()
    for t in range(blocks):
        turn_values(0, t)

    def advance(h, dot, shift):
        tops = []
        for c in range(2 * tokens // CHUNK):
            part = pl.ds(c * CHUNK, CHUNK)
            weights[part, :] = jnp.exp2(scores[part, :] * RATE - shift).astype(jnp.bfloat16)
            source = k if c * CHUNK < tokens else kp
            fresh = dot(source[pl.ds((c * CHUNK) % tokens, CHUNK), cols(h)])
            scores[part, :] = fresh
            tops.append(jnp.max(fresh, axis=0, keepdims=True))
        return functools.reduce(jnp.maximum, tops) * RATE

    def gather(h, top):
        total = jnp.dot(vt[h], weights[...], preferred_element_type=jnp.float32)
        sums = total[HD : HD + 1]
        return total[:HD] * (1.0 / sums), top + jnp.log2(sums)

    def merge(s):
        u = jnp.maximum(s - LAG, 0)
        near_lse, far_lse = own_lse[u], px_lse[jnp.maximum(s - LAG + 1, 0)] - shift
        top = jnp.maximum(near_lse, far_lse)
        near_part, far_part = jnp.exp2(near_lse - top), jnp.exp2(far_lse - top)
        scale = 1.0 / (near_part + far_part)
        mixed = own[u] * (near_part * scale) + px[s].astype(jnp.float32) * (far_part * scale)
        stage[u] = mixed.T.astype(jnp.bfloat16)

    def await_slot(s):
        remote(first.at[0], px.at[s], x_send.at[s], x_recv.at[s], across).wait_recv()

        @pl.when(s >= LAG)
        def with_lse():
            lse_slot(s - LAG).wait_recv()

    def pass_on(u):
        @pl.when(lax.rem(u, blocks) < blocks - 1)
        def away():
            to_seq(u).start()

        @pl.when(lax.rem(u, blocks) == blocks - 1)
        def here():
            to_self(u).start()

    def step(s, carry):
        unit = jnp.minimum(s, units - 1)
        before = jnp.maximum(s - 1, 0)
        h, t = unit // blocks, lax.rem(s, blocks)
        h_before = before // blocks
        h_next = jnp.minimum(h + 1, heads - 1)
        await_slot(s)

        @pl.when(jnp.logical_and(t == 0, s < units))
        def await_head():
            load(1, h).wait()
            to_partner(0, h).wait_recv()

            @pl.when(h + 1 < heads)
            def next_head():
                load(0, h + 1).wait()
                load(2, h + 1).wait()
                to_partner(1, h + 1).wait_recv()

        result, lse = gather(h_before, cross_top[...])
        query_block = px[s]
        cross_top[...] = advance(
            h,
            lambda key: jnp.dot(key, query_block, preferred_element_type=jnp.float32),
            own_top[...],
        )
        ahead = jnp.minimum(before + LAG, units - 1)
        turned = q[rows(ahead), cols(ahead // blocks)].T.astype(jnp.float32)
        pay[before] = (turned * higher + result * lower).astype(jnp.bfloat16)
        pay_lse[before] = lse

        @pl.when(s > 0)
        def answer():
            later_slot(before).start()
            lse_slot(before).start()

        merge(s)
        result, lse = gather(h_before, own_top[...])
        own[before] = result
        own_lse[before] = lse
        own_query = q[rows(unit), cols(h)]
        own_top[...] = advance(
            h,
            lambda key: lax.dot_general(
                key, own_query, (((1,), (1,)), ((), ())), preferred_element_type=jnp.float32
            ),
            cross_top[...],
        )
        turn_values(h_next, t)

        @pl.when(s >= LAG)
        def finished():
            pass_on(s - LAG)

        return carry

    lax.fori_loop(0, units + 1, step, 0)

    def complete(s, carry):
        await_slot(s)
        merge(s)
        pass_on(s - LAG)
        return carry

    lax.fori_loop(units + 1, units + LAG, complete, 0)

    def drain_first(s, carry):
        first_slot(s).wait_send()
        return carry

    lax.fori_loop(0, LAG, drain_first, 0)

    def drain(u, carry):
        later_slot(u).wait_send()
        lse_slot(u).wait_send()

        @pl.when(lax.rem(u, blocks) < blocks - 1)
        def away():
            to_seq(u).wait_send()
            to_seq(u).wait_recv()

        @pl.when(lax.rem(u, blocks) == blocks - 1)
        def here():
            to_self(u).wait()

        return carry

    lax.fori_loop(0, units, drain, 0)

    def drain_partner(h, carry):
        for i in range(2):
            to_partner(i, h).wait_send()
        return carry

    lax.fori_loop(0, heads, drain_partner, 0)


def per_device_fused(queries, keys, values, span_order):
    tokens, width = queries.shape[2], queries.shape[3]
    heads = width // HD
    seq_count = lax.axis_size("seq")
    blocks = tokens // ROWS
    units = heads * blocks
    slots = units + LAG
    bias_rate = 1.0 / (2.0 * span_order.shape[0])
    query, key, value = (a.reshape(tokens, width) for a in (queries, keys, values))
    far = pl.BlockSpec(memory_space=pltpu.HBM)
    dma = pltpu.SemaphoreType.DMA

    def half(*shape):
        return pltpu.VMEM(shape, jnp.bfloat16)

    def full(*shape):
        return pltpu.VMEM(shape, jnp.float32)

    result = pl.pallas_call(
        functools.partial(fused_kernel, heads, bias_rate),
        out_shape=pltpu.VMEM((tokens // seq_count, width * seq_count), jnp.bfloat16),
        in_specs=[pl.BlockSpec(memory_space=pltpu.SMEM), far, far, far],
        out_specs=pl.BlockSpec(memory_space=pltpu.VMEM),
        scratch_shapes=[half(tokens, width)] * 5
        + [half(LAG, HD, ROWS), half(units, HD, ROWS), full(units, 1, ROWS)]
        + [half(slots, HD, ROWS), full(units + 1, 1, ROWS)]
        + [full(units, HD, ROWS), full(units, 1, ROWS), half(units, ROWS, HD)]
        + [half(heads, HD + ONES, 2 * tokens)]
        + [full(2 * tokens, ROWS)]
        + [half(2 * tokens, ROWS)]
        + [full(1, ROWS)] * 2
        + [dma((3, heads)), dma((2, heads)), dma((2, heads)), dma((slots,)), dma((slots,))]
        + [dma((units,))] * 4
        + [dma((heads,))],
        compiler_params=pltpu.CompilerParams(
            collective_id=0, has_side_effects=True, vmem_limit_bytes=60 * 1024 * 1024
        ),
    )(span_order, query, key, value)
    return result.reshape(1, 1, tokens // seq_count, width * seq_count)


def per_device(queries, keys, values, span_order):
    tokens = queries.shape[2]
    seq_count = lax.axis_size("seq")
    fits = (
        lax.axis_size("span") == 2
        and lax.axis_size("head") == 2
        and seq_count == 4
        and tokens == seq_count * ROWS
        and queries.shape[3] % HD == 0
    )
    run = per_device_fused if fits else per_device_general
    return run(queries, keys, values, span_order)


def solution(mesh):
    return jax.shard_map(
        per_device,
        mesh=mesh,
        in_specs=(
            P(("rep", "span"), "head", None, "seq"),
            P(("rep", "span"), "head", None, "seq"),
            P(("rep", "span"), "head", None, "seq"),
            P("rep"),
        ),
        out_specs=P(("rep", "span"), "head", "seq", None),
        check_vma=False,
    )
```

```python
import functools
import math

import jax
import jax.numpy as jnp
from jax import lax
from jax.experimental import pallas as pl
from jax.experimental.pallas import tpu as pltpu
from jax.sharding import PartitionSpec as P

HD = 128


def lookup(span_order, block_index):
    table = jnp.arange(span_order.shape[0], dtype=jnp.int32)
    return jnp.sum(
        jnp.where(block_index[:, None] == table[None, :], span_order[None, :], 0), axis=1
    )


def initial(query_heads):
    query_count = query_heads.shape[0]
    local_heads = query_heads.shape[1]
    return (
        jnp.full((local_heads, query_count), -1e30, jnp.float32),
        jnp.zeros((local_heads, query_count), jnp.float32),
        jnp.zeros((local_heads, query_count, HD), jnp.float32),
    )


def attend(running, query_heads, key_piece, value_piece, block_span, own_span, bias_rate):
    block_count = key_piece.shape[0]
    piece_rows = key_piece.shape[1]
    local_heads = key_piece.shape[2] // HD
    key_count = block_count * piece_rows
    score_scale = 1.0 / math.sqrt(HD)
    key_spans = jnp.repeat(block_span, piece_rows)
    allowed = key_spans <= own_span
    distance_bias = (own_span - key_spans).astype(jnp.float32) * jnp.float32(bias_rate)
    block_size = 1024
    block_total = key_count // block_size
    key_blocks = key_piece.reshape(block_total, block_size, local_heads, HD)
    value_blocks = value_piece.reshape(block_total, block_size, local_heads, HD)
    allow_blocks = allowed.reshape(block_total, block_size)
    bias_blocks = distance_bias.reshape(block_total, block_size)

    def advance(status, block_item):
        key_block, value_block, allow_block, bias_block = block_item
        maxima, totals, weighted = status
        scores = (
            jnp.einsum("qhd,khd->hqk", query_heads, key_block, preferred_element_type=jnp.float32)
            * score_scale
        )
        scores = scores - bias_block[None, None, :]
        scores = jnp.where(allow_block[None, None, :], scores, jnp.float32(-1e30))
        new_max = jnp.maximum(maxima, jnp.max(scores, axis=2))
        weights = jnp.where(
            allow_block[None, None, :], jnp.exp(scores - new_max[:, :, None]), 0.0
        ).astype(jnp.bfloat16)
        shrink = jnp.exp(maxima - new_max)
        totals = totals * shrink + jnp.sum(weights.astype(jnp.float32), axis=2)
        weighted = weighted * shrink[:, :, None] + jnp.einsum(
            "hqk,khd->hqd", weights, value_block, preferred_element_type=jnp.float32
        )
        return ((new_max, totals, weighted), None)

    running, unused = lax.scan(
        advance, running, (key_blocks, value_blocks, allow_blocks, bias_blocks)
    )
    return running


def finish(running):
    maxima, totals, weighted = running
    local_heads = weighted.shape[0]
    query_count = weighted.shape[1]
    output = (weighted / totals[:, :, None]).transpose(1, 0, 2)
    return output.reshape(1, 1, query_count, local_heads * HD).astype(jnp.bfloat16)


def per_device_general(queries, keys, values, span_order):
    half_rows = queries.shape[2]
    local_width = queries.shape[3]
    local_heads = local_width // HD
    halves = lax.axis_size("head")
    bias_rate = 1.0 / (2.0 * span_order.shape[0])
    own_span = lookup(span_order, jnp.reshape(lax.axis_index("span"), (1,)))[0]
    query_heads = queries.reshape(half_rows, local_heads, HD)
    pieces = (
        lax.all_gather(keys, ("span", "head"), axis=0, tiled=True),
        lax.all_gather(values, ("span", "head"), axis=0, tiled=True),
    )
    count = pieces[0].shape[0]
    block_index = jnp.arange(count, dtype=jnp.int32) // halves
    key_piece = pieces[0].reshape(count, half_rows, local_width)
    value_piece = pieces[1].reshape(count, half_rows, local_width)
    running = attend(
        initial(query_heads),
        query_heads,
        key_piece,
        value_piece,
        lookup(span_order, block_index),
        own_span,
        bias_rate,
    )
    result = finish(running)
    return lax.all_to_all(result, "seq", split_axis=2, concat_axis=3, tiled=True)


MESH = pl.DeviceIdType.MESH
ROWS = 256
CHUNK = 256
LAG = 4
ONES = 16
LOG2E = 1.4426950408889634
RATE = LOG2E / math.sqrt(HD)


def fused_kernel(
    heads, bias_rate, order_ref, q_in, k_in, v_in, out_ref,
    q, k, v, kp, vp, first, pay, pay_lse, px, px_lse, own, own_lse, stage, vt,
    scores, weights, cross_top, own_top,
    in_sem, p_send, p_recv, x_send, x_recv, l_send, l_recv, z_send, z_recv, keep_sem,
):
    rep, span = lax.axis_index("rep"), lax.axis_index("span")
    seq, core = lax.axis_index("seq"), lax.axis_index("head")
    partner = (rep, span, seq, 1 - core)
    across = (rep, 1 - span, seq, core)
    tokens, width = q.shape
    blocks = tokens // ROWS
    units = heads * blocks

    def cols(h):
        return pl.ds(pl.multiple_of(h * HD, HD), HD)

    def target(u):
        far = blocks - 1 - lax.rem(u, blocks)
        return 2 * lax.rem(seq // 2 + far // 2, 2) + lax.rem(seq + far, 2)

    def rows(u):
        return pl.ds(pl.multiple_of(target(u) * ROWS, ROWS), ROWS)

    def load(i, h):
        src, dst = ((q_in, q), (k_in, k), (v_in, v))[i]
        return pltpu.make_async_copy(src.at[:, cols(h)], dst.at[:, cols(h)], in_sem.at[i, h])

    def remote(src, dst, send, recv, device):
        return pltpu.make_async_remote_copy(
            src_ref=src, dst_ref=dst, send_sem=send, recv_sem=recv,
            device_id=device, device_id_type=MESH,
        )

    def to_partner(i, h):
        src, dst = ((k_in, kp), (v_in, vp))[i]
        return remote(
            src.at[:, cols(h)], dst.at[:, cols(h)], p_send.at[i, h], p_recv.at[i, h], partner
        )

    def first_slot(s):
        return remote(first.at[s], px.at[s], x_send.at[s], x_recv.at[s], across)

    def later_slot(u):
        s = u + LAG
        return remote(pay.at[u], px.at[s], x_send.at[s], x_recv.at[s], across)

    def lse_slot(u):
        return remote(pay_lse.at[u], px_lse.at[u + 1], l_send.at[u], l_recv.at[u], across)

    def out_cols(u):
        return pl.ds(pl.multiple_of(seq * width + (u // blocks) * HD, HD), HD)

    def to_seq(u):
        return remote(
            stage.at[u], out_ref.at[:, out_cols(u)], z_send.at[u], z_recv.at[u],
            (rep, span, target(u), core),
        )

    def to_self(u):
        return pltpu.make_async_copy(stage.at[u], out_ref.at[:, out_cols(u)], keep_sem.at[u // blocks])

    barrier = pltpu.get_barrier_semaphore()
    peers = [partner, across]
    for far in range(1, blocks):
        there = 2 * lax.rem(seq // 2 + far // 2, 2) + lax.rem(seq + far, 2)
        peers.append((rep, span, there, core))
    for peer in peers:
        pl.semaphore_signal(barrier, inc=1, device_id=peer, device_id_type=MESH)

    def fetch(h):
        for i in range(3):
            load(i, h).start()

    def share(h):
        for i in range(2):
            to_partner(i, h).start()

    fetch(0)
    load(0, 0).wait()
    first[0] = q[rows(0), cols(0)].T
    pl.semaphore_wait(barrier, len(peers))

    first_slot(0).start()
    share(0)
    for s in range(1, LAG):
        first[s] = q[rows(s), cols(0)].T
        first_slot(s).start()
    fetch(1)
    share(1)

    difference = order_ref[span] - order_ref[1 - span]
    higher = jnp.minimum(jnp.maximum(difference, 0), 1).astype(jnp.float32)
    lower = 1.0 - higher
    shift = difference.astype(jnp.float32) * (bias_rate * LOG2E) * higher + lower * 1e30

    vt[:, HD:, :] = jnp.ones((heads, ONES, 2 * tokens), jnp.bfloat16)

    def turn_values(h, t):
        here = pl.ds(pl.multiple_of(t * ROWS, ROWS), ROWS)
        there = pl.ds(pl.multiple_of(tokens + t * ROWS, ROWS), ROWS)
        vt[h, :HD, here] = v[here, cols(h)].T
        vt[h, :HD, there] = vp[here, cols(h)].T

    load(2, 0).wait()
    to_partner(1, 0).wait_recv()
    for t in range(blocks):
        turn_values(0, t)

    def advance(h, dot, shift):
        tops = []
        for c in range(2 * tokens // CHUNK):
            part = pl.ds(c * CHUNK, CHUNK)
            weights[part, :] = jnp.exp2(scores[part, :] * RATE - shift).astype(jnp.bfloat16)
            source = k if c * CHUNK < tokens else kp
            fresh = dot(source[pl.ds((c * CHUNK) % tokens, CHUNK), cols(h)])
            scores[part, :] = fresh
            tops.append(jnp.max(fresh, axis=0, keepdims=True))
        return functools.reduce(jnp.maximum, tops) * RATE

    def gather(h, top):
        total = jnp.dot(vt[h], weights[...], preferred_element_type=jnp.float32)
        sums = total[HD : HD + 1]
        return total[:HD] * (1.0 / sums), top + jnp.log2(sums)

    def merge(s):
        u = jnp.maximum(s - LAG, 0)
        near_lse, far_lse = own_lse[u], px_lse[jnp.maximum(s - LAG + 1, 0)] - shift
        top = jnp.maximum(near_lse, far_lse)
        near_part, far_part = jnp.exp2(near_lse - top), jnp.exp2(far_lse - top)
        scale = 1.0 / (near_part + far_part)
        mixed = own[u] * (near_part * scale) + px[s].astype(jnp.float32) * (far_part * scale)
        stage[u] = mixed.T.astype(jnp.bfloat16)

    def await_slot(s):
        remote(first.at[0], px.at[s], x_send.at[s], x_recv.at[s], across).wait_recv()

        @pl.when(s >= LAG)
        def with_lse():
            lse_slot(s - LAG).wait_recv()

    def pass_on(u):
        @pl.when(lax.rem(u, blocks) < blocks - 1)
        def away():
            to_seq(u).start()

        @pl.when(lax.rem(u, blocks) == blocks - 1)
        def here():
            to_self(u).start()

    def step(s, carry):
        unit = jnp.minimum(s, units - 1)
        before = jnp.maximum(s - 1, 0)
        h, t = unit // blocks, lax.rem(s, blocks)
        h_before = before // blocks
        h_next = jnp.minimum(h + 1, heads - 1)
        await_slot(s)

        @pl.when(jnp.logical_and(t == 0, s < units))
        def await_head():
            @pl.when(h + 2 < heads)
            def bring():
                fetch(h + 2)
                share(h + 2)

            load(1, h).wait()
            to_partner(0, h).wait_recv()

            @pl.when(h + 1 < heads)
            def next_head():
                load(0, h + 1).wait()
                load(2, h + 1).wait()
                to_partner(1, h + 1).wait_recv()

        result, lse = gather(h_before, cross_top[...])
        query_block = px[s]
        cross_top[...] = advance(
            h,
            lambda key: jnp.dot(key, query_block, preferred_element_type=jnp.float32),
            own_top[...],
        )
        ahead = jnp.minimum(before + LAG, units - 1)
        turned = q[rows(ahead), cols(ahead // blocks)].T.astype(jnp.float32)
        pay[before] = (turned * higher + result * lower).astype(jnp.bfloat16)
        pay_lse[before] = lse

        @pl.when(s > 0)
        def answer():
            later_slot(before).start()
            lse_slot(before).start()

        merge(s)
        result, lse = gather(h_before, own_top[...])
        own[before] = result
        own_lse[before] = lse
        own_query = q[rows(unit), cols(h)]
        own_top[...] = advance(
            h,
            lambda key: lax.dot_general(
                key, own_query, (((1,), (1,)), ((), ())), preferred_element_type=jnp.float32
            ),
            cross_top[...],
        )
        turn_values(h_next, t)

        @pl.when(s >= LAG)
        def finished():
            pass_on(s - LAG)

        return carry

    lax.fori_loop(0, units + 1, step, 0)

    def complete(s, carry):
        await_slot(s)
        merge(s)
        pass_on(s - LAG)
        return carry

    lax.fori_loop(units + 1, units + LAG, complete, 0)

    def drain_first(s, carry):
        first_slot(s).wait_send()
        return carry

    lax.fori_loop(0, LAG, drain_first, 0)

    def drain(u, carry):
        later_slot(u).wait_send()
        lse_slot(u).wait_send()

        @pl.when(lax.rem(u, blocks) < blocks - 1)
        def away():
            to_seq(u).wait_send()
            to_seq(u).wait_recv()

        @pl.when(lax.rem(u, blocks) == blocks - 1)
        def here():
            to_self(u).wait()

        return carry

    lax.fori_loop(0, units, drain, 0)

    def drain_partner(h, carry):
        for i in range(2):
            to_partner(i, h).wait_send()
        return carry

    lax.fori_loop(0, heads, drain_partner, 0)


def per_device_fused(queries, keys, values, span_order):
    tokens, width = queries.shape[2], queries.shape[3]
    heads = width // HD
    seq_count = lax.axis_size("seq")
    blocks = tokens // ROWS
    units = heads * blocks
    slots = units + LAG
    bias_rate = 1.0 / (2.0 * span_order.shape[0])
    query, key, value = (a.reshape(tokens, width) for a in (queries, keys, values))
    far = pl.BlockSpec(memory_space=pltpu.HBM)
    dma = pltpu.SemaphoreType.DMA

    def half(*shape):
        return pltpu.VMEM(shape, jnp.bfloat16)

    def full(*shape):
        return pltpu.VMEM(shape, jnp.float32)

    result = pl.pallas_call(
        functools.partial(fused_kernel, heads, bias_rate),
        out_shape=pltpu.VMEM((tokens // seq_count, width * seq_count), jnp.bfloat16),
        in_specs=[pl.BlockSpec(memory_space=pltpu.SMEM), far, far, far],
        out_specs=pl.BlockSpec(memory_space=pltpu.VMEM),
        scratch_shapes=[half(tokens, width)] * 5
        + [half(LAG, HD, ROWS), half(units, HD, ROWS), full(units, 1, ROWS)]
        + [half(slots, HD, ROWS), full(units + 1, 1, ROWS)]
        + [full(units, HD, ROWS), full(units, 1, ROWS), half(units, ROWS, HD)]
        + [half(heads, HD + ONES, 2 * tokens)]
        + [full(2 * tokens, ROWS)]
        + [half(2 * tokens, ROWS)]
        + [full(1, ROWS)] * 2
        + [dma((3, heads)), dma((2, heads)), dma((2, heads)), dma((slots,)), dma((slots,))]
        + [dma((units,))] * 4
        + [dma((heads,))],
        compiler_params=pltpu.CompilerParams(
            collective_id=0, has_side_effects=True, vmem_limit_bytes=60 * 1024 * 1024
        ),
    )(span_order, query, key, value)
    return result.reshape(1, 1, tokens // seq_count, width * seq_count)


def per_device(queries, keys, values, span_order):
    tokens = queries.shape[2]
    seq_count = lax.axis_size("seq")
    fits = (
        lax.axis_size("span") == 2
        and lax.axis_size("head") == 2
        and seq_count == 4
        and tokens == seq_count * ROWS
        and queries.shape[3] % HD == 0
        and queries.shape[3] >= 2 * HD
    )
    run = per_device_fused if fits else per_device_general
    return run(queries, keys, values, span_order)


def solution(mesh):
    return jax.shard_map(
        per_device,
        mesh=mesh,
        in_specs=(
            P(("rep", "span"), "head", None, "seq"),
            P(("rep", "span"), "head", None, "seq"),
            P(("rep", "span"), "head", None, "seq"),
            P("rep"),
        ),
        out_specs=P(("rep", "span"), "head", "seq", None),
        check_vma=False,
    )
```

```python
import functools
import math

import jax
import jax.numpy as jnp
from jax import lax
from jax.experimental import pallas as pl
from jax.experimental.pallas import tpu as pltpu
from jax.sharding import PartitionSpec as P

HD = 128


def lookup(span_order, block_index):
    table = jnp.arange(span_order.shape[0], dtype=jnp.int32)
    return jnp.sum(
        jnp.where(block_index[:, None] == table[None, :], span_order[None, :], 0), axis=1
    )


def initial(query_heads):
    query_count = query_heads.shape[0]
    local_heads = query_heads.shape[1]
    return (
        jnp.full((local_heads, query_count), -1e30, jnp.float32),
        jnp.zeros((local_heads, query_count), jnp.float32),
        jnp.zeros((local_heads, query_count, HD), jnp.float32),
    )


def attend(running, query_heads, key_piece, value_piece, block_span, own_span, bias_rate):
    block_count = key_piece.shape[0]
    piece_rows = key_piece.shape[1]
    local_heads = key_piece.shape[2] // HD
    key_count = block_count * piece_rows
    score_scale = 1.0 / math.sqrt(HD)
    key_spans = jnp.repeat(block_span, piece_rows)
    allowed = key_spans <= own_span
    distance_bias = (own_span - key_spans).astype(jnp.float32) * jnp.float32(bias_rate)
    block_size = 1024
    block_total = key_count // block_size
    key_blocks = key_piece.reshape(block_total, block_size, local_heads, HD)
    value_blocks = value_piece.reshape(block_total, block_size, local_heads, HD)
    allow_blocks = allowed.reshape(block_total, block_size)
    bias_blocks = distance_bias.reshape(block_total, block_size)

    def advance(status, block_item):
        key_block, value_block, allow_block, bias_block = block_item
        maxima, totals, weighted = status
        scores = (
            jnp.einsum("qhd,khd->hqk", query_heads, key_block, preferred_element_type=jnp.float32)
            * score_scale
        )
        scores = scores - bias_block[None, None, :]
        scores = jnp.where(allow_block[None, None, :], scores, jnp.float32(-1e30))
        new_max = jnp.maximum(maxima, jnp.max(scores, axis=2))
        weights = jnp.where(
            allow_block[None, None, :], jnp.exp(scores - new_max[:, :, None]), 0.0
        ).astype(jnp.bfloat16)
        shrink = jnp.exp(maxima - new_max)
        totals = totals * shrink + jnp.sum(weights.astype(jnp.float32), axis=2)
        weighted = weighted * shrink[:, :, None] + jnp.einsum(
            "hqk,khd->hqd", weights, value_block, preferred_element_type=jnp.float32
        )
        return ((new_max, totals, weighted), None)

    running, unused = lax.scan(
        advance, running, (key_blocks, value_blocks, allow_blocks, bias_blocks)
    )
    return running


def finish(running):
    maxima, totals, weighted = running
    local_heads = weighted.shape[0]
    query_count = weighted.shape[1]
    output = (weighted / totals[:, :, None]).transpose(1, 0, 2)
    return output.reshape(1, 1, query_count, local_heads * HD).astype(jnp.bfloat16)


def per_device_general(queries, keys, values, span_order):
    half_rows = queries.shape[2]
    local_width = queries.shape[3]
    local_heads = local_width // HD
    halves = lax.axis_size("head")
    bias_rate = 1.0 / (2.0 * span_order.shape[0])
    own_span = lookup(span_order, jnp.reshape(lax.axis_index("span"), (1,)))[0]
    query_heads = queries.reshape(half_rows, local_heads, HD)
    pieces = (
        lax.all_gather(keys, ("span", "head"), axis=0, tiled=True),
        lax.all_gather(values, ("span", "head"), axis=0, tiled=True),
    )
    count = pieces[0].shape[0]
    block_index = jnp.arange(count, dtype=jnp.int32) // halves
    key_piece = pieces[0].reshape(count, half_rows, local_width)
    value_piece = pieces[1].reshape(count, half_rows, local_width)
    running = attend(
        initial(query_heads),
        query_heads,
        key_piece,
        value_piece,
        lookup(span_order, block_index),
        own_span,
        bias_rate,
    )
    result = finish(running)
    return lax.all_to_all(result, "seq", split_axis=2, concat_axis=3, tiled=True)


MESH = pl.DeviceIdType.MESH
ROWS = 256
CHUNK = 128
LAG = 4
ONES = 16
LOG2E = 1.4426950408889634
RATE = LOG2E / math.sqrt(HD)


def fused_kernel(
    heads, bias_rate, order_ref, q_in, k_in, v_in, out_ref,
    q, k, v, kp, vp, first, pay, pay_lse, px, px_lse, own, own_lse, stage, vt,
    scores, weights, cross_top, own_top,
    in_sem, p_send, p_recv, x_send, x_recv, l_send, l_recv, z_send, z_recv, keep_sem,
):
    rep, span = lax.axis_index("rep"), lax.axis_index("span")
    seq, core = lax.axis_index("seq"), lax.axis_index("head")
    partner = (rep, span, seq, 1 - core)
    across = (rep, 1 - span, seq, core)
    tokens, width = q.shape
    blocks = tokens // ROWS
    units = heads * blocks

    def cols(h):
        return pl.ds(pl.multiple_of(h * HD, HD), HD)

    def target(u):
        far = blocks - 1 - lax.rem(u, blocks)
        return 2 * lax.rem(seq // 2 + far // 2, 2) + lax.rem(seq + far, 2)

    def rows(u):
        return pl.ds(pl.multiple_of(target(u) * ROWS, ROWS), ROWS)

    def load(i, h):
        src, dst = ((q_in, q), (k_in, k), (v_in, v))[i]
        return pltpu.make_async_copy(src.at[:, cols(h)], dst.at[:, cols(h)], in_sem.at[i, h])

    def remote(src, dst, send, recv, device):
        return pltpu.make_async_remote_copy(
            src_ref=src, dst_ref=dst, send_sem=send, recv_sem=recv,
            device_id=device, device_id_type=MESH,
        )

    def to_partner(i, h):
        src, dst = ((k_in, kp), (v_in, vp))[i]
        return remote(
            src.at[:, cols(h)], dst.at[:, cols(h)], p_send.at[i, h], p_recv.at[i, h], partner
        )

    def first_slot(s):
        return remote(first.at[s], px.at[s], x_send.at[s], x_recv.at[s], across)

    def later_slot(u):
        s = u + LAG
        return remote(pay.at[u], px.at[s], x_send.at[s], x_recv.at[s], across)

    def lse_slot(u):
        return remote(pay_lse.at[u], px_lse.at[u + 1], l_send.at[u], l_recv.at[u], across)

    def out_cols(u):
        return pl.ds(pl.multiple_of(seq * width + (u // blocks) * HD, HD), HD)

    def to_seq(u):
        return remote(
            stage.at[u], out_ref.at[:, out_cols(u)], z_send.at[u], z_recv.at[u],
            (rep, span, target(u), core),
        )

    def to_self(u):
        return pltpu.make_async_copy(stage.at[u], out_ref.at[:, out_cols(u)], keep_sem.at[u // blocks])

    def start_loads(h, carry):
        for i in range(3):
            load(i, h).start()
        return carry

    lax.fori_loop(0, heads, start_loads, 0)

    barrier = pltpu.get_barrier_semaphore()
    peers = [partner, across]
    for far in range(1, blocks):
        there = 2 * lax.rem(seq // 2 + far // 2, 2) + lax.rem(seq + far, 2)
        peers.append((rep, span, there, core))
    for peer in peers:
        pl.semaphore_signal(barrier, inc=1, device_id=peer, device_id_type=MESH)

    load(0, 0).wait()
    for s in range(LAG):
        first[s] = q[rows(s), cols(0)].T
    pl.semaphore_wait(barrier, len(peers))

    first_slot(0).start()
    for i in range(2):
        to_partner(i, 0).start()
    for s in range(1, LAG):
        first_slot(s).start()

    def start_partner(h, carry):
        for i in range(2):
            to_partner(i, h).start()
        return carry

    lax.fori_loop(1, heads, start_partner, 0)

    difference = order_ref[span] - order_ref[1 - span]
    higher = jnp.minimum(jnp.maximum(difference, 0), 1).astype(jnp.float32)
    lower = 1.0 - higher
    shift = difference.astype(jnp.float32) * (bias_rate * LOG2E) * higher + lower * 1e30

    vt[:, HD:, :] = jnp.ones((heads, ONES, 2 * tokens), jnp.bfloat16)

    def turn_values(h, t):
        here = pl.ds(pl.multiple_of(t * ROWS, ROWS), ROWS)
        there = pl.ds(pl.multiple_of(tokens + t * ROWS, ROWS), ROWS)
        vt[h, :HD, here] = v[here, cols(h)].T
        vt[h, :HD, there] = vp[here, cols(h)].T

    load(2, 0).wait()
    to_partner(1, 0).wait_recv()
    for t in range(blocks):
        turn_values(0, t)

    def advance(h, dot, shift):
        tops = []
        for c in range(2 * tokens // CHUNK):
            part = pl.ds(c * CHUNK, CHUNK)
            weights[part, :] = jnp.exp2(scores[part, :] * RATE - shift).astype(jnp.bfloat16)
            source = k if c * CHUNK < tokens else kp
            fresh = dot(source[pl.ds((c * CHUNK) % tokens, CHUNK), cols(h)])
            scores[part, :] = fresh
            tops.append(jnp.max(fresh, axis=0, keepdims=True))
        return functools.reduce(jnp.maximum, tops) * RATE

    def gather(h, top):
        total = jnp.dot(vt[h], weights[...], preferred_element_type=jnp.float32)
        sums = total[HD : HD + 1]
        return total[:HD] * (1.0 / sums), top + jnp.log2(sums)

    def merge(s):
        u = jnp.maximum(s - LAG, 0)
        near_lse, far_lse = own_lse[u], px_lse[jnp.maximum(s - LAG + 1, 0)] - shift
        top = jnp.maximum(near_lse, far_lse)
        near_part, far_part = jnp.exp2(near_lse - top), jnp.exp2(far_lse - top)
        scale = 1.0 / (near_part + far_part)
        mixed = own[u] * (near_part * scale) + px[s].astype(jnp.float32) * (far_part * scale)
        stage[u] = mixed.T.astype(jnp.bfloat16)

    def await_slot(s):
        remote(first.at[0], px.at[s], x_send.at[s], x_recv.at[s], across).wait_recv()

        @pl.when(s >= LAG)
        def with_lse():
            lse_slot(s - LAG).wait_recv()

    def pass_on(u):
        @pl.when(lax.rem(u, blocks) < blocks - 1)
        def away():
            to_seq(u).start()

        @pl.when(lax.rem(u, blocks) == blocks - 1)
        def here():
            to_self(u).start()

    def step(s, carry):
        unit = jnp.minimum(s, units - 1)
        before = jnp.maximum(s - 1, 0)
        h, t = unit // blocks, lax.rem(s, blocks)
        h_before = before // blocks
        h_next = jnp.minimum(h + 1, heads - 1)
        await_slot(s)

        @pl.when(jnp.logical_and(t == 0, s < units))
        def await_head():
            load(1, h).wait()
            to_partner(0, h).wait_recv()

            @pl.when(h + 1 < heads)
            def next_head():
                load(0, h + 1).wait()
                load(2, h + 1).wait()
                to_partner(1, h + 1).wait_recv()

        result, lse = gather(h_before, cross_top[...])
        query_block = px[s]
        cross_top[...] = advance(
            h,
            lambda key: jnp.dot(key, query_block, preferred_element_type=jnp.float32),
            own_top[...],
        )
        ahead = jnp.minimum(before + LAG, units - 1)
        turned = q[rows(ahead), cols(ahead // blocks)].T.astype(jnp.float32)
        pay[before] = (turned * higher + result * lower).astype(jnp.bfloat16)
        pay_lse[before] = lse

        @pl.when(s > 0)
        def answer():
            later_slot(before).start()
            lse_slot(before).start()

        merge(s)
        result, lse = gather(h_before, own_top[...])
        own[before] = result
        own_lse[before] = lse
        own_query = q[rows(unit), cols(h)]
        own_top[...] = advance(
            h,
            lambda key: lax.dot_general(
                key, own_query, (((1,), (1,)), ((), ())), preferred_element_type=jnp.float32
            ),
            cross_top[...],
        )
        turn_values(h_next, t)

        @pl.when(s >= LAG)
        def finished():
            pass_on(s - LAG)

        return carry

    lax.fori_loop(0, units + 1, step, 0)

    def complete(s, carry):
        await_slot(s)
        merge(s)
        pass_on(s - LAG)
        return carry

    lax.fori_loop(units + 1, units + LAG, complete, 0)

    def drain_first(s, carry):
        first_slot(s).wait_send()
        return carry

    lax.fori_loop(0, LAG, drain_first, 0)

    def drain(u, carry):
        later_slot(u).wait_send()
        lse_slot(u).wait_send()

        @pl.when(lax.rem(u, blocks) < blocks - 1)
        def away():
            to_seq(u).wait_send()
            to_seq(u).wait_recv()

        @pl.when(lax.rem(u, blocks) == blocks - 1)
        def here():
            to_self(u).wait()

        return carry

    lax.fori_loop(0, units, drain, 0)

    def drain_partner(h, carry):
        for i in range(2):
            to_partner(i, h).wait_send()
        return carry

    lax.fori_loop(0, heads, drain_partner, 0)


def per_device_fused(queries, keys, values, span_order):
    tokens, width = queries.shape[2], queries.shape[3]
    heads = width // HD
    seq_count = lax.axis_size("seq")
    blocks = tokens // ROWS
    units = heads * blocks
    slots = units + LAG
    bias_rate = 1.0 / (2.0 * span_order.shape[0])
    query, key, value = (a.reshape(tokens, width) for a in (queries, keys, values))
    far = pl.BlockSpec(memory_space=pltpu.HBM)
    dma = pltpu.SemaphoreType.DMA

    def half(*shape):
        return pltpu.VMEM(shape, jnp.bfloat16)

    def full(*shape):
        return pltpu.VMEM(shape, jnp.float32)

    result = pl.pallas_call(
        functools.partial(fused_kernel, heads, bias_rate),
        out_shape=pltpu.VMEM((tokens // seq_count, width * seq_count), jnp.bfloat16),
        in_specs=[pl.BlockSpec(memory_space=pltpu.SMEM), far, far, far],
        out_specs=pl.BlockSpec(memory_space=pltpu.VMEM),
        scratch_shapes=[half(tokens, width)] * 5
        + [half(LAG, HD, ROWS), half(units, HD, ROWS), full(units, 1, ROWS)]
        + [half(slots, HD, ROWS), full(units + 1, 1, ROWS)]
        + [full(units, HD, ROWS), full(units, 1, ROWS), half(units, ROWS, HD)]
        + [half(heads, HD + ONES, 2 * tokens)]
        + [full(2 * tokens, ROWS)]
        + [half(2 * tokens, ROWS)]
        + [full(1, ROWS)] * 2
        + [dma((3, heads)), dma((2, heads)), dma((2, heads)), dma((slots,)), dma((slots,))]
        + [dma((units,))] * 4
        + [dma((heads,))],
        compiler_params=pltpu.CompilerParams(
            collective_id=0, has_side_effects=True, vmem_limit_bytes=60 * 1024 * 1024
        ),
    )(span_order, query, key, value)
    return result.reshape(1, 1, tokens // seq_count, width * seq_count)


def per_device(queries, keys, values, span_order):
    tokens = queries.shape[2]
    seq_count = lax.axis_size("seq")
    fits = (
        lax.axis_size("span") == 2
        and lax.axis_size("head") == 2
        and seq_count == 4
        and tokens == seq_count * ROWS
        and queries.shape[3] % HD == 0
    )
    run = per_device_fused if fits else per_device_general
    return run(queries, keys, values, span_order)


def solution(mesh):
    return jax.shard_map(
        per_device,
        mesh=mesh,
        in_specs=(
            P(("rep", "span"), "head", None, "seq"),
            P(("rep", "span"), "head", None, "seq"),
            P(("rep", "span"), "head", None, "seq"),
            P("rep"),
        ),
        out_specs=P(("rep", "span"), "head", "seq", None),
        check_vma=False,
    )
```
